32 devices in a mesh: dp: 16 (over z, y, core), tensor: 2 (over x).
Axes of the slice: x: 2, y: 2, z: 4, core: 2. Of those that a mesh axis runs over, the one named last changes fastest.
Arguments:
- tokens: bfloat16 [32, 448, 1024], P('dp'), may hold values from -6 to 6
- encoded: bfloat16 [32, 1500, 1024], P('dp'), may hold values from -6 to 6
- cotangent: bfloat16 [32, 448, 1024], P('dp'), may hold values from -6 to 6
- self_gain: bfloat16 [1024], replicated, may hold values from 0.5 to 1.5
- self_shift: bfloat16 [1024], replicated, may hold values from -1.75 to 1.75
- self_query: bfloat16 [1024, 1024], P(None, 'tensor'), may hold values from -0.25 to 0.25
- self_query_bias: bfloat16 [1024], P('tensor'), may hold values from -1.75 to 1.75
- self_key: bfloat16 [1024, 1024], P(None, 'tensor'), may hold values from -0.1875 to 0.1875
- self_value: bfloat16 [1024, 1024], P(None, 'tensor'), may hold values from -0.1875 to 0.1875
- self_value_bias: bfloat16 [1024], P('tensor'), may hold values from -1.75 to 1.75
- self_mixer: bfloat16 [1024, 1024], P('tensor'), may hold values from -0.5 to 0.5
- self_mixer_bias: bfloat16 [1024], replicated, may hold values from -1.75 to 1.75
- cross_gain: bfloat16 [1024], replicated, may hold values from 0.5 to 1.5
- cross_shift: bfloat16 [1024], replicated, may hold values from -1.75 to 1.75
- cross_query: bfloat16 [1024, 1024], P(None, 'tensor'), may hold values from -0.25 to 0.25
- cross_query_bias: bfloat16 [1024], P('tensor'), may hold values from -1.75 to 1.75
- cross_key: bfloat16 [1024, 1024], P(None, 'tensor'), may hold values from -0.1875 to 0.1875
- cross_value: bfloat16 [1024, 1024], P(None, 'tensor'), may hold values from -0.1875 to 0.1875
- cross_value_bias: bfloat16 [1024], P('tensor'), may hold values from -1.75 to 1.75
- cross_mixer: bfloat16 [1024, 1024], P('tensor'), may hold values from -0.75 to 0.75
- cross_mixer_bias: bfloat16 [1024], replicated, may hold values from -1.75 to 1.75
- feed_gain: bfloat16 [1024], replicated, may hold values from 0.5 to 1.5
- feed_shift: bfloat16 [1024], replicated, may hold values from -1.75 to 1.75
- expand_weight: bfloat16 [1024, 4096], P(None, 'tensor'), may hold values from -0.1875 to 0.1875
- expand_bias: bfloat16 [4096], P('tensor'), may hold values from -3 to 3
- reduce_weight: bfloat16 [4096, 1024], P('tensor'), may hold values from -0.125 to 0.125
- reduce_bias: bfloat16 [1024], replicated, may hold values from -1.75 to 1.75
Outputs:
- output: float32 [32, 448, 1024], P('dp')
- grad_tokens: float32 [32, 448, 1024], P('dp')
- grad_encoded: float32 [32, 1500, 1024], P('dp', None, 'tensor')
- grad_self_gain: float32 [1024], replicated
- grad_self_shift: float32 [1024], replicated
- grad_self_query: float32 [1024, 1024], P(None, 'tensor')
- grad_self_query_bias: float32 [1024], P('tensor')
- grad_self_key: float32 [1024, 1024], P(None, 'tensor')
- grad_self_value: float32 [1024, 1024], P(None, 'tensor')
- grad_self_value_bias: float32 [1024], P('tensor')
- grad_self_mixer: float32 [1024, 1024], P('tensor')
- grad_self_mixer_bias: float32 [1024], replicated
- grad_cross_gain: float32 [1024], replicated
- grad_cross_shift: float32 [1024], replicated
- grad_cross_query: float32 [1024, 1024], P(None, 'tensor')
- grad_cross_query_bias: float32 [1024], P('tensor')
- grad_cross_key: float32 [1024, 1024], P(None, 'tensor')
- grad_cross_value: float32 [1024, 1024], P(None, 'tensor')
- grad_cross_value_bias: float32 [1024], P('tensor')
- grad_cross_mixer: float32 [1024, 1024], P('tensor')
- grad_cross_mixer_bias: float32 [1024], replicated
- grad_feed_gain: float32 [1024], replicated
- grad_feed_shift: float32 [1024], replicated
- grad_expand_weight: float32 [1024, 4096], P(None, 'tensor')
- grad_expand_bias: float32 [4096], P('tensor')
- grad_reduce_weight: float32 [4096, 1024], P('tensor')
- grad_reduce_bias: float32 [1024], replicated
The draws below stay inside these ranges and needn't reach their ends.
All inputs are finite; a program needn't handle non-finite values.
Results may differ from the reference program's by a relative error of at most 0.022.
Values may be sent and summed in bfloat16 or wider, within the bound.
No kernel may reach another device: no remote copies, remote signals or barrier semaphores. Data moves between devices by JAX's collectives and lax.ppermute only.
A program may use at most 256 MiB of HBM per device.

```python
import math
import jax
import jax.numpy as jnp
from jax import lax

D = 1024
HEADS = 16
HEAD = 64
FF = 4096
LEN = 448
FRAMES = 1500
CLIPS = 32


def steps_of(rng, shape, shards, low, high):
    factor_of = 1.0
    for position, blocks in shards:
        heights = jax.random.uniform(jax.random.fold_in(jax.random.fold_in(rng, 6), position), (blocks,), jnp.float32, low / len(shards), high / len(shards))
        factor_of = factor_of * jnp.repeat(jnp.exp(heights), shape[position] // blocks).reshape((-1,) + (1,) * (len(shape) - 1 - position))
    return factor_of


def scatter_about(stream_key, shape, scale, most, split=(), kind=jnp.bfloat16):
    level = steps_of(stream_key, shape, split, -0.22, 0.18) if split else 1.0
    values = jax.random.normal(stream_key, shape, jnp.float32) * scale * level
    return jnp.minimum(jnp.maximum(values, -most), most).astype(kind)


def setup_inputs(seed: int = 0) -> dict:
    streams_of = jax.random.split(jax.random.key(seed), 28)
    tokens = scatter_about(streams_of[0], (CLIPS, LEN, D), 1.0, 6.0, ((0, 16),))
    encoded = scatter_about(streams_of[1], (CLIPS, FRAMES, D), 1.0, 6.0, ((0, 16),))
    cotangent = scatter_about(streams_of[2], (CLIPS, LEN, D), 1.0, 6.0, ((0, 16),))
    self_gain = jnp.clip(1.0 + 0.1 * jax.random.normal(streams_of[3], (D,), jnp.float32), 0.5, 1.5).astype(jnp.bfloat16)
    self_shift = scatter_about(streams_of[4], (D,), 0.3, 1.75)
    self_query = scatter_about(streams_of[5], (D, D), (D // 2) ** -0.5, 0.25, ((1, 2),))
    self_query_bias = scatter_about(streams_of[6], (D,), 0.3, 1.75, ((0, 2),))
    self_key = scatter_about(streams_of[7], (D, D), D ** -0.5, 0.1875, ((1, 2),))
    self_value = scatter_about(streams_of[8], (D, D), D ** -0.5, 0.1875, ((1, 2),))
    self_value_bias = scatter_about(streams_of[9], (D,), 0.3, 1.75, ((0, 2),))
    self_mixer = scatter_about(streams_of[10], (D, D), (D // 8) ** -0.5, 0.5, ((0, 2),))
    self_mixer_bias = scatter_about(streams_of[11], (D,), 0.3, 1.75)
    cross_gain = jnp.clip(1.0 + 0.1 * jax.random.normal(streams_of[12], (D,), jnp.float32), 0.5, 1.5).astype(jnp.bfloat16)
    cross_shift = scatter_about(streams_of[13], (D,), 0.3, 1.75)
    cross_query = scatter_about(streams_of[14], (D, D), (D // 2) ** -0.5, 0.25, ((1, 2),))
    cross_query_bias = scatter_about(streams_of[15], (D,), 0.3, 1.75, ((0, 2),))
    cross_key = scatter_about(streams_of[16], (D, D), D ** -0.5, 0.1875, ((1, 2),))
    cross_value = scatter_about(streams_of[17], (D, D), D ** -0.5, 0.1875, ((1, 2),))
    cross_value_bias = scatter_about(streams_of[18], (D,), 0.3, 1.75, ((0, 2),))
    cross_mixer = scatter_about(streams_of[19], (D, D), (D // 16) ** -0.5, 0.75, ((0, 2),))
    cross_mixer_bias = scatter_about(streams_of[20], (D,), 0.3, 1.75)
    feed_gain = jnp.clip(1.0 + 0.1 * jax.random.normal(streams_of[21], (D,), jnp.float32), 0.5, 1.5).astype(jnp.bfloat16)
    feed_shift = scatter_about(streams_of[22], (D,), 0.3, 1.75)
    expand_weight = scatter_about(streams_of[23], (D, FF), D ** -0.5, 0.1875, ((1, 2),))
    expand_bias = scatter_about(streams_of[24], (FF,), 0.5, 3.0, ((0, 2),))
    reduce_weight = scatter_about(streams_of[25], (FF, D), (FF // 2) ** -0.5, 0.125, ((0, 2),))
    reduce_bias = scatter_about(streams_of[26], (D,), 0.3, 1.75)
    return {"tokens": tokens, "encoded": encoded, "cotangent": cotangent, "self_gain": self_gain, "self_shift": self_shift, "self_query": self_query, "self_query_bias": self_query_bias, "self_key": self_key, "self_value": self_value, "self_value_bias": self_value_bias, "self_mixer": self_mixer, "self_mixer_bias": self_mixer_bias, "cross_gain": cross_gain, "cross_shift": cross_shift, "cross_query": cross_query, "cross_query_bias": cross_query_bias, "cross_key": cross_key, "cross_value": cross_value, "cross_value_bias": cross_value_bias, "cross_mixer": cross_mixer, "cross_mixer_bias": cross_mixer_bias, "feed_gain": feed_gain, "feed_shift": feed_shift, "expand_weight": expand_weight, "expand_bias": expand_bias, "reduce_weight": reduce_weight, "reduce_bias": reduce_bias}


@jax.custom_vjp
def low(v):
    return lax.optimization_barrier(v.astype(jnp.bfloat16)).astype(jnp.float32)

@jax.custom_vjp
def low_back(v):
    return v

def low_keep(v):
    return (low(v), None)

def low_pass(kept, grad):
    return (grad,)

def back_keep(v):
    return (v, None)

def back_low(kept, grad):
    return (low(grad),)
low.defvjp(low_keep, low_pass)
low_back.defvjp(back_keep, back_low)

def rounded_both(value):
    return low(low_back(value))

def product(left, right):
    return jnp.dot(left, right, precision=lax.Precision.HIGHEST, preferred_element_type=jnp.float32)

def normalize(values, norm_gain, norm_shift):
    row_mean = lax.optimization_barrier(jnp.mean(values, axis=-1, keepdims=True))
    centered = values - row_mean
    spread = lax.optimization_barrier(jnp.mean(centered * centered, axis=-1, keepdims=True))
    return centered * lax.rsqrt(spread + 1e-05) * norm_gain + norm_shift

def attention(queries, key_rows, value_rows, causal):
    length = queries.shape[0]
    count = key_rows.shape[0]
    query_heads = queries.reshape(length, HEADS, HEAD)
    key_heads = key_rows.reshape(count, HEADS, HEAD)
    value_heads = value_rows.reshape(count, HEADS, HEAD)
    scores = jnp.einsum('lhe,khe->hlk', query_heads, key_heads, precision=lax.Precision.HIGHEST) * (1.0 / math.sqrt(HEAD))
    scores = low_back(scores)
    if causal:
        row_index = lax.broadcasted_iota(jnp.int32, (length, count), 0)
        col_index = lax.broadcasted_iota(jnp.int32, (length, count), 1)
        scores = jnp.where((col_index <= row_index)[None], scores, -1e+30)
    probs = jax.nn.softmax(scores, axis=-1)
    mixture = jnp.einsum('hlk,khe->lhe', low(probs), value_heads, precision=lax.Precision.HIGHEST)
    return rounded_both(mixture.reshape(length, D))

def group_sum(inputs, weight):
    return low_back(product(inputs, weight))

def layer(params, tokens, encoded):
    self_gain, self_shift, self_query, self_query_bias, self_key, self_value, self_value_bias, self_mixer, self_mixer_bias, cross_gain, cross_shift, cross_query, cross_query_bias, cross_key, cross_value, cross_value_bias, cross_mixer, cross_mixer_bias, feed_gain, feed_shift, expand_weight, expand_bias, reduce_weight, reduce_bias = params
    attn_in = low(normalize(tokens, self_gain, self_shift))
    queries = rounded_both(product(attn_in, self_query) + self_query_bias)
    key_rows = rounded_both(product(attn_in, self_key))
    value_rows = rounded_both(product(attn_in, self_value) + self_value_bias)
    self_mixture = attention(queries, key_rows, value_rows, True)
    hidden_one = tokens + group_sum(self_mixture, self_mixer) + self_mixer_bias
    cross_in = low(normalize(hidden_one, cross_gain, cross_shift))
    cross_queries = rounded_both(product(cross_in, cross_query) + cross_query_bias)
    cross_keys = rounded_both(product(encoded, cross_key))
    cross_values = rounded_both(product(encoded, cross_value) + cross_value_bias)
    cross_mixture = attention(cross_queries, cross_keys, cross_values, False)
    hidden_two = hidden_one + group_sum(cross_mixture, cross_mixer) + cross_mixer_bias
    feed_in = low(normalize(hidden_two, feed_gain, feed_shift))
    preact = low_back(product(feed_in, expand_weight) + expand_bias)
    activated = low(jax.nn.gelu(preact, approximate=False))
    return hidden_two + group_sum(activated, reduce_weight) + reduce_bias

def reference(tokens, encoded, cotangent, self_gain, self_shift, self_query, self_query_bias, self_key, self_value, self_value_bias, self_mixer, self_mixer_bias, cross_gain, cross_shift, cross_query, cross_query_bias, cross_key, cross_value, cross_value_bias, cross_mixer, cross_mixer_bias, feed_gain, feed_shift, expand_weight, expand_bias, reduce_weight, reduce_bias):
    params = tuple((piece.astype(jnp.float32) for piece in (self_gain, self_shift, self_query, self_query_bias, self_key, self_value, self_value_bias, self_mixer, self_mixer_bias, cross_gain, cross_shift, cross_query, cross_query_bias, cross_key, cross_value, cross_value_bias, cross_mixer, cross_mixer_bias, feed_gain, feed_shift, expand_weight, expand_bias, reduce_weight, reduce_bias)))

    def clip_step(totals, inputs):
        clip_tokens, clip_frames, clip_grad = inputs
        result, pull = jax.vjp(layer, params, clip_tokens, clip_frames)
        grads, grad_input, grad_frames = pull(clip_grad)
        totals = jax.tree.map(lambda left, right: left + right, totals, grads)
        return (totals, (result, grad_input, grad_frames))
    zeros = jax.tree.map(jnp.zeros_like, params)
    totals, stacked = lax.scan(clip_step, zeros, (tokens.astype(jnp.float32), encoded.astype(jnp.float32), cotangent.astype(jnp.float32)))
    return (stacked[0], stacked[1], stacked[2], totals[0], totals[1], totals[2], totals[3], totals[4], totals[5], totals[6], totals[7], totals[8], totals[9], totals[10], totals[11], totals[12], totals[13], totals[14], totals[15], totals[16], totals[17], totals[18], totals[19], totals[20], totals[21], totals[22], totals[23])
```

```python
import math

import jax
import jax.numpy as jnp
from jax import lax
from jax.sharding import PartitionSpec as P

HEAD = 64
EPSILON = 1e-05
F32 = jnp.float32
BF16 = jnp.bfloat16


def normalize(values, norm_gain, norm_shift):
    row_mean = jnp.mean(values, axis=-1, keepdims=True)
    centered = values - row_mean
    spread = jnp.mean(centered * centered, axis=-1, keepdims=True)
    inverse = lax.rsqrt(spread + EPSILON)
    normed = centered * inverse
    return (normed * norm_gain + norm_shift, normed, inverse)


def normalize_back(grad_out, normed, inverse, norm_gain):
    scaled = grad_out * norm_gain
    centre = jnp.mean(scaled, axis=-1, keepdims=True)
    row_along = jnp.mean(scaled * normed, axis=-1, keepdims=True)
    grad_in = inverse * (scaled - centre - normed * row_along)
    return (grad_in, jnp.sum(grad_out * normed, axis=0), jnp.sum(grad_out, axis=0))


def scores_of(queries, key_heads, causal):
    scaling = 1.0 / math.sqrt(queries.shape[-1])
    scores = jnp.einsum("lhe,khe->hlk", queries, key_heads, preferred_element_type=F32) * scaling
    if causal:
        row_index = lax.broadcasted_iota(jnp.int32, scores.shape[-2:], 0)
        col_index = lax.broadcasted_iota(jnp.int32, scores.shape[-2:], 1)
        scores = jnp.where(col_index <= row_index, scores, -1e30)
    return scores


def attend(queries, key_heads, value_heads, causal):
    scores = scores_of(queries, key_heads, causal)
    highest = jnp.max(scores, axis=-1, keepdims=True)
    denominator = jnp.sum(jnp.exp(scores - highest), axis=-1, keepdims=True)
    logsum = highest + jnp.log(denominator)
    probs = jnp.exp(scores - logsum)
    mixture = jnp.einsum(
        "hlk,khe->lhe", probs.astype(BF16), value_heads, preferred_element_type=F32
    )
    return (mixture.astype(BF16), logsum)


def attend_back(grad_mixture, queries, key_heads, value_heads, logsum, causal):
    scaling = 1.0 / math.sqrt(queries.shape[-1])
    probs = jnp.exp(scores_of(queries, key_heads, causal) - logsum)
    grad_probs = jnp.einsum("lhe,khe->hlk", grad_mixture, value_heads, preferred_element_type=F32)
    row_dot = jnp.sum(grad_probs * probs, axis=-1, keepdims=True)
    grad_scores = (probs * (grad_probs - row_dot)).astype(BF16)
    grad_queries = (
        jnp.einsum("hlk,khe->lhe", grad_scores, key_heads, preferred_element_type=F32) * scaling
    ).astype(BF16)
    grad_keys = (
        jnp.einsum("hlk,lhe->khe", grad_scores, queries, preferred_element_type=F32) * scaling
    ).astype(BF16)
    grad_values = jnp.einsum(
        "hlk,lhe->khe", probs.astype(BF16), grad_mixture, preferred_element_type=F32
    ).astype(BF16)
    return (grad_queries, grad_keys, grad_values)


def project(inputs, weight):
    return jnp.dot(inputs, weight, preferred_element_type=F32)


def project_back(grads, weight):
    return jnp.einsum("lc,dc->ld", grads, weight, preferred_element_type=F32)


def weight_grad(inputs, grads):
    left = jnp.concatenate(inputs, axis=0)
    right = jnp.concatenate(grads, axis=0)
    return jnp.einsum("ld,lc->dc", left, right, preferred_element_type=F32).astype(BF16)


def column_sum(grads):
    return jnp.sum(grads.astype(F32), axis=0)


def tensor_sum(partial):
    if lax.axis_size("tensor") != 2:
        return lax.psum(partial, "tensor")
    mine = lax.optimization_barrier(partial.astype(BF16))
    other = lax.ppermute(mine, "tensor", [(0, 1), (1, 0)])
    return mine.astype(F32) + other.astype(F32)


def dp_sum(grads):
    share = lax.psum_scatter(grads, "dp", scatter_dimension=0, tiled=True)
    return lax.all_gather(share, "dp", axis=0, tiled=True)


def local(
    tokens,
    encoded,
    cotangent,
    self_gain,
    self_shift,
    self_query,
    self_query_bias,
    self_key,
    self_value,
    self_value_bias,
    self_mixer,
    self_mixer_bias,
    cross_gain,
    cross_shift,
    cross_query,
    cross_query_bias,
    cross_key,
    cross_value,
    cross_value_bias,
    cross_mixer,
    cross_mixer_bias,
    feed_gain,
    feed_shift,
    expand_weight,
    expand_bias,
    reduce_weight,
    reduce_bias,
):
    clips, length, width = tokens.shape
    frames = encoded.shape[1]
    local_width = self_query.shape[1]
    head_count = local_width // HEAD
    gain_one = self_gain.astype(F32)
    gain_two = cross_gain.astype(F32)
    gain_three = feed_gain.astype(F32)
    each = range(clips)

    def heads(values):
        return values.reshape(values.shape[0], head_count, HEAD)

    def flat(values):
        return values.reshape(values.shape[0], local_width)

    source, normed_one, inverse_one, attn_in = [], [], [], []
    self_queries, self_keys, self_values = [], [], []
    self_mixture, self_logsum, self_sum = [], [], []
    cross_keys, cross_values = [], []
    for i in each:
        source.append(tokens[i].astype(F32))
        normed, plain, inverse = normalize(source[i], gain_one, self_shift.astype(F32))
        normed_one.append(plain)
        inverse_one.append(inverse)
        attn_in.append(normed.astype(BF16))
        self_queries.append(
            (project(attn_in[i], self_query) + self_query_bias.astype(F32)).astype(BF16)
        )
        self_keys.append(project(attn_in[i], self_key).astype(BF16))
        self_values.append(
            (project(attn_in[i], self_value) + self_value_bias.astype(F32)).astype(BF16)
        )
        mixed, logsum = attend(heads(self_queries[i]), heads(self_keys[i]), heads(self_values[i]), True)
        self_mixture.append(flat(mixed))
        self_logsum.append(logsum)
        self_sum.append(tensor_sum(project(self_mixture[i], self_mixer)))
    for i in each:
        cross_keys.append(project(encoded[i], cross_key).astype(BF16))
        cross_values.append(
            (project(encoded[i], cross_value) + cross_value_bias.astype(F32)).astype(BF16)
        )

    hidden_one, normed_two, inverse_two, cross_in = [], [], [], []
    cross_queries, cross_mixture, cross_logsum, cross_sum = [], [], [], []
    for i in each:
        hidden_one.append(source[i] + self_sum[i] + self_mixer_bias.astype(F32))
        normed, plain, inverse = normalize(hidden_one[i], gain_two, cross_shift.astype(F32))
        normed_two.append(plain)
        inverse_two.append(inverse)
        cross_in.append(normed.astype(BF16))
        cross_queries.append(
            (project(cross_in[i], cross_query) + cross_query_bias.astype(F32)).astype(BF16)
        )
        mixed, logsum = attend(
            heads(cross_queries[i]), heads(cross_keys[i]), heads(cross_values[i]), False
        )
        cross_mixture.append(flat(mixed))
        cross_logsum.append(logsum)
        cross_sum.append(tensor_sum(project(cross_mixture[i], cross_mixer)))

    hidden_two, normed_three, inverse_three, feed_in = [], [], [], []
    activated, grad_preact, feed_grad, feed_sum = [], [], [], []
    for i in each:
        hidden_two.append(hidden_one[i] + cross_sum[i] + cross_mixer_bias.astype(F32))
        normed, plain, inverse = normalize(hidden_two[i], gain_three, feed_shift.astype(F32))
        normed_three.append(plain)
        inverse_three.append(inverse)
        feed_in.append(normed.astype(BF16))
        preact = project(feed_in[i], expand_weight) + expand_bias.astype(F32)
        grad_activated = project_back(cotangent[i], reduce_weight)
        cdf = 0.5 * (1.0 + lax.erf(preact * (1.0 / math.sqrt(2.0))))
        density = jnp.exp(-0.5 * preact * preact) * (1.0 / math.sqrt(2.0 * math.pi))
        activated.append((preact * cdf).astype(BF16))
        grad_preact.append((grad_activated * (cdf + preact * density)).astype(BF16))
        feed_grad.append(tensor_sum(project_back(grad_preact[i], expand_weight)))
    for i in each:
        feed_sum.append(tensor_sum(project(activated[i], reduce_weight)))
    output = [hidden_two[i] + feed_sum[i] + reduce_bias.astype(F32) for i in each]
    grad_out = [cotangent[i].astype(F32) for i in each]
    grad_reduce_weight = dp_sum(weight_grad(activated, [cotangent[i] for i in each]))
    grad_expand_weight = dp_sum(weight_grad(feed_in, grad_preact))
    grad_reduce_bias = sum(jnp.sum(grad_out[i], axis=0) for i in each)
    grad_expand_bias = sum(column_sum(grad_preact[i]) for i in each)

    grad_two, two_rounded, feed_gains, feed_shifts = [], [], [], []
    cross_query_grad, cross_key_grad, cross_value_grad = [], [], []
    cross_grad = []
    for i in each:
        norm_grad, part_gain, part_shift = normalize_back(
            feed_grad[i], normed_three[i], inverse_three[i], gain_three
        )
        feed_gains.append(part_gain)
        feed_shifts.append(part_shift)
        grad_two.append(grad_out[i] + norm_grad)
        two_rounded.append(grad_two[i].astype(BF16))
        grad_cross_mixture = project_back(two_rounded[i], cross_mixer).astype(BF16)
        query_grad, key_grad, value_grad = attend_back(
            heads(grad_cross_mixture),
            heads(cross_queries[i]),
            heads(cross_keys[i]),
            heads(cross_values[i]),
            cross_logsum[i],
            False,
        )
        cross_query_grad.append(flat(query_grad))
        cross_key_grad.append(flat(key_grad))
        cross_value_grad.append(flat(value_grad))
        cross_grad.append(tensor_sum(project_back(cross_query_grad[i], cross_query)))
    grad_cross_mixer = dp_sum(weight_grad(cross_mixture, two_rounded))
    grad_cross_query = dp_sum(weight_grad(cross_in, cross_query_grad))
    frames_in = [encoded[i] for i in each]
    grad_cross_key = dp_sum(weight_grad(frames_in, cross_key_grad))
    grad_cross_value = dp_sum(weight_grad(frames_in, cross_value_grad))
    part_cross_mixer_bias = sum(jnp.sum(grad_two[i], axis=0) for i in each)
    grad_cross_query_bias = sum(column_sum(cross_query_grad[i]) for i in each)
    grad_cross_value_bias = sum(column_sum(cross_value_grad[i]) for i in each)

    grad_one, one_rounded, cross_gains, cross_shifts = [], [], [], []
    query_grads, key_grads, value_grads, self_grad = [], [], [], []
    for i in each:
        norm_grad, part_gain, part_shift = normalize_back(
            cross_grad[i], normed_two[i], inverse_two[i], gain_two
        )
        cross_gains.append(part_gain)
        cross_shifts.append(part_shift)
        grad_one.append(grad_two[i] + norm_grad)
        one_rounded.append(grad_one[i].astype(BF16))
        grad_self_mixture = project_back(one_rounded[i], self_mixer).astype(BF16)
        query_grad, key_grad, value_grad = attend_back(
            heads(grad_self_mixture),
            heads(self_queries[i]),
            heads(self_keys[i]),
            heads(self_values[i]),
            self_logsum[i],
            True,
        )
        query_grads.append(flat(query_grad))
        key_grads.append(flat(key_grad))
        value_grads.append(flat(value_grad))
        self_terms = (
            project_back(query_grads[i], self_query)
            + project_back(key_grads[i], self_key)
            + project_back(value_grads[i], self_value)
        )
        self_grad.append(tensor_sum(self_terms))
    grad_self_mixer = dp_sum(weight_grad(self_mixture, one_rounded))
    grad_self_query = dp_sum(weight_grad(attn_in, query_grads))
    grad_self_key = dp_sum(weight_grad(attn_in, key_grads))
    grad_self_value = dp_sum(weight_grad(attn_in, value_grads))
    part_self_mixer_bias = sum(jnp.sum(grad_one[i], axis=0) for i in each)
    grad_self_query_bias = sum(column_sum(query_grads[i]) for i in each)
    grad_self_value_bias = sum(column_sum(value_grads[i]) for i in each)

    grad_encoded = []
    members = lax.axis_size("tensor")
    share = width // members
    for i in each:
        if members == 2:
            me = lax.axis_index("tensor")

            def terms(part):
                rows_key = lax.dynamic_slice_in_dim(cross_key, part * share, share, 0)
                rows_value = lax.dynamic_slice_in_dim(cross_value, part * share, share, 0)
                return project_back(cross_key_grad[i], rows_key) + project_back(
                    cross_value_grad[i], rows_value
                )

            other = lax.ppermute(terms(1 - me).astype(BF16), "tensor", [(0, 1), (1, 0)])
            grad_encoded.append(terms(me) + other.astype(F32))
        else:
            frame_terms = project_back(cross_key_grad[i], cross_key) + project_back(
                cross_value_grad[i], cross_value
            )
            grad_encoded.append(
                lax.psum_scatter(frame_terms, "tensor", scatter_dimension=1, tiled=True)
            )

    self_gains, self_shifts, grad_tokens = [], [], []
    for i in each:
        norm_grad, part_gain, part_shift = normalize_back(
            self_grad[i], normed_one[i], inverse_one[i], gain_one
        )
        self_gains.append(part_gain)
        self_shifts.append(part_shift)
        grad_tokens.append(grad_one[i] + norm_grad)

    vectors = [
        sum(self_gains),
        sum(self_shifts),
        part_self_mixer_bias,
        sum(cross_gains),
        sum(cross_shifts),
        part_cross_mixer_bias,
        sum(feed_gains),
        sum(feed_shifts),
        grad_reduce_bias,
        grad_self_query_bias,
        grad_self_value_bias,
        grad_cross_query_bias,
        grad_cross_value_bias,
        grad_expand_bias,
    ]
    summed = lax.psum(jnp.concatenate(vectors), "dp")
    pieces, offset = [], 0
    for piece in vectors:
        pieces.append(summed[offset : offset + piece.size])
        offset = offset + piece.size
    return (
        jnp.stack(output),
        jnp.stack(grad_tokens),
        jnp.stack(grad_encoded),
        pieces[0],
        pieces[1],
        grad_self_query.astype(F32),
        pieces[9],
        grad_self_key.astype(F32),
        grad_self_value.astype(F32),
        pieces[10],
        grad_self_mixer.astype(F32),
        pieces[2],
        pieces[3],
        pieces[4],
        grad_cross_query.astype(F32),
        pieces[11],
        grad_cross_key.astype(F32),
        grad_cross_value.astype(F32),
        pieces[12],
        grad_cross_mixer.astype(F32),
        pieces[5],
        pieces[6],
        pieces[7],
        grad_expand_weight.astype(F32),
        pieces[13],
        grad_reduce_weight.astype(F32),
        pieces[8],
    )


def solution(mesh):
    rows = P("dp", None, None)
    column, row, part = P(None, "tensor"), P("tensor", None), P("tensor")
    return jax.shard_map(
        local,
        mesh=mesh,
        in_specs=(
            rows,
            rows,
            rows,
            P(),
            P(),
            column,
            part,
            column,
            column,
            part,
            row,
            P(),
            P(),
            P(),
            column,
            part,
            column,
            column,
            part,
            row,
            P(),
            P(),
            P(),
            column,
            part,
            row,
            P(),
        ),
        out_specs=(
            rows,
            rows,
            P("dp", None, "tensor"),
            P(),
            P(),
            column,
            part,
            column,
            column,
            part,
            row,
            P(),
            P(),
            P(),
            column,
            part,
            column,
            column,
            part,
            row,
            P(),
            P(),
            P(),
            column,
            part,
            row,
            P(),
        ),
        check_vma=False,
    )
```

```python
import functools
import math

import jax
import jax.numpy as jnp
from jax import lax
from jax.experimental import pallas as pl
from jax.experimental.pallas import tpu as pltpu
from jax.sharding import PartitionSpec as P

HEAD = 64
PAIR = 2 * HEAD
EPSILON = 1e-05
F32 = jnp.float32
BF16 = jnp.bfloat16
SCALING = 1.0 / math.sqrt(HEAD)
LOG2E = 1.0 / math.log(2.0)

NN = (((1,), (0,)), ((), ()))
NT = (((1,), (1,)), ((), ()))
TN = (((0,), (0,)), ((), ()))

(
    SELF_GAIN,
    SELF_SHIFT,
    SELF_MIXER_BIAS,
    CROSS_GAIN,
    CROSS_SHIFT,
    CROSS_MIXER_BIAS,
    FEED_GAIN,
    FEED_SHIFT,
    REDUCE_BIAS,
) = range(9)
SELF_QUERY_BIAS, SELF_VALUE_BIAS, CROSS_QUERY_BIAS, CROSS_VALUE_BIAS = range(4)


def dot(left, right, dims):
    return lax.dot_general(left, right, dims, preferred_element_type=F32)


def row_of(table, index):
    return table[index : index + 1, :]


def whole(shape):
    return pl.BlockSpec(shape, lambda *step: (0,) * len(shape))


def clip_of(array, clip):
    return pl.BlockSpec((None,) + array.shape[1:], lambda *step: (clip, 0, 0))


def call(kernel, grid, in_specs, outs, scratch=(), flops=0, traffic=0, aliases=None, name=None):
    return pl.pallas_call(
        kernel,
        grid=grid,
        in_specs=in_specs,
        out_specs=[spec for _, _, spec in outs],
        out_shape=[jax.ShapeDtypeStruct(shape, dtype) for shape, dtype, _ in outs],
        scratch_shapes=scratch,
        input_output_aliases=aliases or {},
        cost_estimate=pl.CostEstimate(
            flops=int(flops), bytes_accessed=int(traffic), transcendentals=0
        ),
        name=name,
    )


def norm_stats(values):
    mean = jnp.mean(values, axis=1, keepdims=True)
    centered = values - mean
    spread = jnp.mean(centered * centered, axis=1, keepdims=True)
    inverse = lax.rsqrt(spread + EPSILON)
    return centered * inverse, inverse


def norm_back(grad, values, gain):
    normed, inverse = norm_stats(values)
    scaled = grad * gain
    centre = jnp.mean(scaled, axis=1, keepdims=True)
    along = jnp.mean(scaled * normed, axis=1, keepdims=True)
    grad_in = inverse * (scaled - centre - normed * along)
    return (
        grad_in,
        jnp.sum(grad * normed, axis=0, keepdims=True),
        jnp.sum(grad, axis=0, keepdims=True),
    )


def both(own_ref, other_ref):
    return own_ref[...].astype(F32) + other_ref[...].astype(F32)


def lanes_of(head):
    lane = lax.broadcasted_iota(jnp.int32, (1, PAIR), 1)
    return lane // HEAD == head


def attend_pair(queries, keys, values, valid, weights_ref, inverse_ref):
    mixture = None
    for head in range(2):
        mask = lanes_of(head)
        scores = dot(jnp.where(mask, queries, 0), keys, NT)
        if valid is not None:
            scores = jnp.where(valid, scores, -1e30)
        highest = jnp.max(scores, axis=1, keepdims=True)
        weights = jnp.exp2((scores - highest) * (SCALING * LOG2E))
        inverse = 1.0 / jnp.sum(weights, axis=1, keepdims=True)
        rounded = weights.astype(BF16)
        weights_ref[head] = rounded
        inverse_ref[head] = inverse
        mixed = dot(rounded, values, NN) * inverse
        mixture = mixed if head == 0 else jnp.where(mask, mixed, mixture)
    return mixture.astype(BF16)


def attend_pair_back(grad, queries, keys, values, mixture, weights_ref, inverse_ref):
    grad_wide, mixture_wide = grad.astype(F32), mixture.astype(F32)
    grad_queries = grad_keys = grad_values = None
    for head in range(2):
        mask = lanes_of(head)
        inverse = inverse_ref[head]
        along = jnp.sum(jnp.where(mask, grad_wide * mixture_wide, 0.0), axis=1, keepdims=True)
        grad_probs = dot(jnp.where(mask, grad, 0), values, NT)
        weights = weights_ref[head]
        grad_scores = (weights.astype(F32) * ((grad_probs - along) * (inverse * SCALING))).astype(
            BF16
        )
        part_queries = dot(grad_scores, keys, NN)
        part_keys = dot(grad_scores, jnp.where(mask, queries, 0), TN)
        part_values = dot(weights, jnp.where(mask, grad_wide * inverse, 0.0).astype(BF16), TN)
        if head == 0:
            grad_queries, grad_keys, grad_values = part_queries, part_keys, part_values
        else:
            grad_queries = jnp.where(mask, part_queries, grad_queries)
            grad_keys = grad_keys + part_keys
            grad_values = grad_values + part_values
    return grad_queries.astype(BF16), grad_keys.astype(BF16), grad_values.astype(BF16)


def pair_columns(ref, base, pair):
    return ref[:, pl.ds(pl.multiple_of(base + pair * PAIR, PAIR), PAIR)]


def self_forward_kernel(
    tokens_ref,
    table_ref,
    biases_ref,
    query_ref,
    key_ref,
    value_ref,
    mixer_ref,
    attn_in_ref,
    heads_ref,
    mixture_ref,
    weights_ref,
    inverse_ref,
    part_ref,
):
    step = pl.program_id(0)
    width = query_ref.shape[1]

    @pl.when(step == 0)
    def _():
        normed, _ = norm_stats(tokens_ref[...].astype(F32))
        attn_in = (normed * row_of(table_ref, SELF_GAIN) + row_of(table_ref, SELF_SHIFT)).astype(
            BF16
        )
        attn_in_ref[...] = attn_in
        queries = dot(attn_in, query_ref[...], NN) + row_of(biases_ref, SELF_QUERY_BIAS)
        heads_ref[:, :width] = queries.astype(BF16)
        heads_ref[:, width : 2 * width] = dot(attn_in, key_ref[...], NN).astype(BF16)
        values = dot(attn_in, value_ref[...], NN) + row_of(biases_ref, SELF_VALUE_BIAS)
        heads_ref[:, 2 * width :] = values.astype(BF16)

    length = tokens_ref.shape[0]
    row = lax.broadcasted_iota(jnp.int32, (length, length), 0)
    column = lax.broadcasted_iota(jnp.int32, (length, length), 1)
    mixture_ref[:, pl.ds(pl.multiple_of(step * PAIR, PAIR), PAIR)] = attend_pair(
        pair_columns(heads_ref, 0, step),
        pair_columns(heads_ref, width, step),
        pair_columns(heads_ref, 2 * width, step),
        column <= row,
        weights_ref,
        inverse_ref,
    )

    @pl.when(step == pl.num_programs(0) - 1)
    def _():
        part_ref[...] = dot(mixture_ref[...], mixer_ref[...], NN).astype(BF16)


def self_forward(clip, tokens, table, biases, query, key, value, mixer):
    _, length, model = tokens.shape
    width = query.shape[1]
    pairs = width // PAIR
    return call(
        self_forward_kernel,
        (pairs,),
        [clip_of(tokens, clip)]
        + [whole(x.shape) for x in (table, biases, query, key, value, mixer)],
        [
            ((length, model), BF16, whole((length, model))),
            ((length, 3 * width), BF16, whole((length, 3 * width))),
            ((length, width), BF16, whole((length, width))),
            (
                (2 * pairs, length, length),
                BF16,
                pl.BlockSpec((2, length, length), lambda g: (g, 0, 0)),
            ),
            ((2 * pairs, length, 1), F32, pl.BlockSpec((2, length, 1), lambda g: (g, 0, 0))),
            ((length, model), BF16, whole((length, model))),
        ],
        flops=8 * length * model * width + 32 * pairs * length * length * PAIR,
        traffic=8 * model * width + 16 * length * model,
        name="self_forward",
    )(tokens, table, biases, query, key, value, mixer)


def frames_kernel(frames, encoded_ref, key_ref, value_ref, biases_ref, out_ref):
    rows, width = encoded_ref.shape[0], key_ref.shape[1]
    row = lax.broadcasted_iota(jnp.int32, (rows, 1), 0) + pl.program_id(1) * rows
    inside = row < frames
    encoded = encoded_ref[...]
    out_ref[:, :width] = jnp.where(inside, dot(encoded, key_ref[...], NN), 0.0).astype(BF16)
    values = dot(encoded, value_ref[...], NN) + row_of(biases_ref, CROSS_VALUE_BIAS)
    out_ref[:, width:] = jnp.where(inside, values, 0.0).astype(BF16)


FRAME_ROWS = 512


def frame_heads(encoded, key, value, biases):
    clips, frames, model = encoded.shape
    width = key.shape[1]
    blocks = -(-frames // FRAME_ROWS)
    (out,) = call(
        functools.partial(frames_kernel, frames),
        (clips, blocks),
        [pl.BlockSpec((None, FRAME_ROWS, model), lambda c, r: (c, r, 0))]
        + [whole(x.shape) for x in (key, value, biases)],
        [
            (
                (clips, blocks * FRAME_ROWS, 2 * width),
                BF16,
                pl.BlockSpec((None, FRAME_ROWS, 2 * width), lambda c, r: (c, r, 0)),
            )
        ],
        flops=4 * clips * frames * model * width,
        traffic=2 * clips * frames * (model + 2 * width),
        name="frame_heads",
    )(encoded, key, value, biases)
    return out


def cross_forward_kernel(
    frames,
    tokens_ref,
    own_ref,
    other_ref,
    table_ref,
    biases_ref,
    query_ref,
    mixer_ref,
    keys_ref,
    values_ref,
    hidden_ref,
    cross_in_ref,
    queries_ref,
    mixture_ref,
    weights_ref,
    inverse_ref,
    part_ref,
):
    step = pl.program_id(0)

    @pl.when(step == 0)
    def _():
        hidden = tokens_ref[...].astype(F32) + both(own_ref, other_ref)
        hidden = hidden + row_of(table_ref, SELF_MIXER_BIAS)
        hidden_ref[...] = hidden
        normed, _ = norm_stats(hidden)
        cross_in = (
            normed * row_of(table_ref, CROSS_GAIN) + row_of(table_ref, CROSS_SHIFT)
        ).astype(BF16)
        cross_in_ref[...] = cross_in
        queries = dot(cross_in, query_ref[...], NN) + row_of(biases_ref, CROSS_QUERY_BIAS)
        queries_ref[...] = queries.astype(BF16)

    length, count = tokens_ref.shape[0], keys_ref.shape[0]
    column = lax.broadcasted_iota(jnp.int32, (length, count), 1)
    mixture_ref[:, pl.ds(pl.multiple_of(step * PAIR, PAIR), PAIR)] = attend_pair(
        pair_columns(queries_ref, 0, step),
        keys_ref[...],
        values_ref[...],
        column < frames,
        weights_ref,
        inverse_ref,
    )

    @pl.when(step == pl.num_programs(0) - 1)
    def _():
        part_ref[...] = dot(mixture_ref[...], mixer_ref[...], NN).astype(BF16)


def cross_forward(clip, frames, tokens, own, other, table, biases, query, mixer, heads):
    _, length, model = tokens.shape
    width = query.shape[1]
    pairs = width // PAIR
    count = heads.shape[1]
    return call(
        functools.partial(cross_forward_kernel, frames),
        (pairs,),
        [clip_of(tokens, clip)]
        + [whole(x.shape) for x in (own, other, table, biases, query, mixer)]
        + [
            pl.BlockSpec((None, count, PAIR), lambda g: (clip, 0, g)),
            pl.BlockSpec((None, count, PAIR), lambda g: (clip, 0, pairs + g)),
        ],
        [
            ((length, model), F32, whole((length, model))),
            ((length, model), BF16, whole((length, model))),
            ((length, width), BF16, whole((length, width))),
            ((length, width), BF16, whole((length, width))),
            (
                (2 * pairs, length, count),
                BF16,
                pl.BlockSpec((2, length, count), lambda g: (g, 0, 0)),
            ),
            ((2 * pairs, length, 1), F32, pl.BlockSpec((2, length, 1), lambda g: (g, 0, 0))),
            ((length, model), BF16, whole((length, model))),
        ],
        flops=4 * length * model * width + 32 * pairs * length * count * PAIR,
        traffic=4 * model * width + 20 * length * model + 4 * pairs * length * count,
        name="cross_forward",
    )(tokens, own, other, table, biases, query, mixer, heads, heads)


def feed_kernel(
    cotangent_ref,
    hidden_ref,
    own_ref,
    other_ref,
    table_ref,
    expand_ref,
    bias_ref,
    reduce_ref,
    hidden_two_ref,
    feed_in_ref,
    activated_ref,
    grad_preact_ref,
    bias_sum_ref,
    cotangent_sum_ref,
    part_ref,
    grad_part_ref,
    total_ref,
    grad_total_ref,
):
    step = pl.program_id(0)

    @pl.when(step == 0)
    def _():
        hidden = hidden_ref[...] + both(own_ref, other_ref) + row_of(table_ref, CROSS_MIXER_BIAS)
        hidden_two_ref[...] = hidden
        normed, _ = norm_stats(hidden)
        feed_in_ref[...] = (
            normed * row_of(table_ref, FEED_GAIN) + row_of(table_ref, FEED_SHIFT)
        ).astype(BF16)
        cotangent_sum_ref[...] = jnp.sum(cotangent_ref[...].astype(F32), axis=0, keepdims=True)

    expand, reduce = expand_ref[...], reduce_ref[...]
    preact = dot(feed_in_ref[...], expand, NN) + bias_ref[...]
    grad_activated = dot(cotangent_ref[...], reduce, NT)
    cdf = 0.5 * (1.0 + lax.erf(preact * math.sqrt(0.5)))
    density = jnp.exp2(preact * preact * (-0.5 * LOG2E)) * (1.0 / math.sqrt(2.0 * math.pi))
    activated = (preact * cdf).astype(BF16)
    grad_preact = (grad_activated * (cdf + preact * density)).astype(BF16)
    activated_ref[...] = activated
    grad_preact_ref[...] = grad_preact
    bias_sum_ref[...] = jnp.sum(grad_preact.astype(F32), axis=0, keepdims=True)
    part = dot(activated, reduce, NN)
    grad_part = dot(grad_preact, expand, NT)

    @pl.when(step == 0)
    def _():
        total_ref[...] = part
        grad_total_ref[...] = grad_part

    @pl.when(step > 0)
    def _():
        total_ref[...] += part
        grad_total_ref[...] += grad_part

    @pl.when(step == pl.num_programs(0) - 1)
    def _():
        part_ref[...] = total_ref[...].astype(BF16)
        grad_part_ref[...] = grad_total_ref[...].astype(BF16)


def feed(clip, cotangent, hidden, own, other, table, expand, bias, reduce):
    _, length, model = cotangent.shape
    inner = expand.shape[1]
    tile = min(512, inner)
    columns = pl.BlockSpec((length, tile), lambda g: (0, g))
    vector = pl.BlockSpec((1, tile), lambda g: (0, g))
    return call(
        feed_kernel,
        (inner // tile,),
        [clip_of(cotangent, clip)]
        + [whole(x.shape) for x in (hidden, own, other, table)]
        + [
            pl.BlockSpec((model, tile), lambda g: (0, g)),
            vector,
            pl.BlockSpec((tile, model), lambda g: (g, 0)),
        ],
        [
            ((length, model), F32, whole((length, model))),
            ((length, model), BF16, whole((length, model))),
            ((length, inner), BF16, columns),
            ((length, inner), BF16, columns),
            ((1, inner), F32, vector),
            ((1, model), F32, whole((1, model))),
            ((length, model), BF16, whole((length, model))),
            ((length, model), BF16, whole((length, model))),
        ],
        scratch=[pltpu.VMEM((length, model), F32)] * 2,
        flops=8 * length * model * inner,
        traffic=4 * model * inner + 4 * length * inner + 20 * length * model,
        name="feed",
    )(cotangent, hidden, own, other, table, expand, bias, reduce)


def cross_backward_kernel(
    frames,
    cotangent_ref,
    own_ref,
    other_ref,
    hidden_ref,
    table_ref,
    query_ref,
    mixer_ref,
    queries_ref,
    mixture_ref,
    keys_ref,
    values_ref,
    weights_ref,
    inverse_ref,
    grad_ref,
    rounded_ref,
    sums_ref,
    query_grad_ref,
    key_grad_ref,
    value_grad_ref,
    head_sums_ref,
    part_ref,
    grad_mixture_ref,
):
    step = pl.program_id(0)
    columns = pl.ds(pl.multiple_of(step * PAIR, PAIR), PAIR)

    @pl.when(step == 0)
    def _():
        norm_grad, gain_sum, shift_sum = norm_back(
            both(own_ref, other_ref), hidden_ref[...], row_of(table_ref, FEED_GAIN)
        )
        grad = cotangent_ref[...].astype(F32) + norm_grad
        grad_ref[...] = grad
        sums_ref[0:1, :] = gain_sum
        sums_ref[1:2, :] = shift_sum
        sums_ref[2:3, :] = jnp.sum(grad, axis=0, keepdims=True)
        rounded = grad.astype(BF16)
        rounded_ref[...] = rounded
        grad_mixture_ref[...] = dot(rounded, mixer_ref[...], NT).astype(BF16)

    query_grad, key_grad, value_grad = attend_pair_back(
        grad_mixture_ref[:, columns],
        queries_ref[...],
        keys_ref[...],
        values_ref[...],
        mixture_ref[...],
        weights_ref,
        inverse_ref,
    )
    query_grad_ref[:, columns] = query_grad
    key_grad_ref[...] = key_grad
    value_grad_ref[...] = value_grad
    head_sums_ref[0:1, columns] = jnp.sum(query_grad.astype(F32), axis=0, keepdims=True)
    head_sums_ref[1:2, columns] = jnp.sum(value_grad.astype(F32), axis=0, keepdims=True)

    @pl.when(step == pl.num_programs(0) - 1)
    def _():
        part_ref[...] = dot(query_grad_ref[...], query_ref[...], NT).astype(BF16)


def cross_backward(
    clip,
    frames,
    cotangent,
    own,
    other,
    hidden,
    table,
    query,
    mixer,
    queries,
    mixture,
    heads,
    weights,
    inverse,
):
    _, length, model = cotangent.shape
    width = query.shape[1]
    pairs = width // PAIR
    count = heads.shape[1]
    pair = pl.BlockSpec((length, PAIR), lambda g: (0, g))
    frame_pair = pl.BlockSpec((count, PAIR), lambda g: (0, g))
    return call(
        functools.partial(cross_backward_kernel, frames),
        (pairs,),
        [clip_of(cotangent, clip)]
        + [whole(x.shape) for x in (own, other, hidden, table, query, mixer)]
        + [
            pair,
            pair,
            pl.BlockSpec((None, count, PAIR), lambda g: (clip, 0, g)),
            pl.BlockSpec((None, count, PAIR), lambda g: (clip, 0, pairs + g)),
            pl.BlockSpec((2, length, count), lambda g: (g, 0, 0)),
            pl.BlockSpec((2, length, 1), lambda g: (g, 0, 0)),
        ],
        [
            ((length, model), F32, whole((length, model))),
            ((length, model), BF16, whole((length, model))),
            ((8, model), F32, whole((8, model))),
            ((length, width), BF16, whole((length, width))),
            ((count, width), BF16, frame_pair),
            ((count, width), BF16, frame_pair),
            ((8, width), F32, whole((8, width))),
            ((length, model), BF16, whole((length, model))),
        ],
        scratch=[pltpu.VMEM((length, width), BF16)],
        flops=4 * length * model * width + 64 * pairs * length * count * PAIR,
        traffic=4 * model * width + 24 * length * model + 4 * pairs * length * count,
        name="cross_backward",
    )(
        cotangent,
        own,
        other,
        hidden,
        table,
        query,
        mixer,
        queries,
        mixture,
        heads,
        heads,
        weights,
        inverse,
    )


def self_backward_kernel(
    grad_two_ref,
    own_ref,
    other_ref,
    hidden_ref,
    table_ref,
    query_ref,
    key_ref,
    value_ref,
    mixer_ref,
    heads_ref,
    mixture_ref,
    weights_ref,
    inverse_ref,
    grad_ref,
    rounded_ref,
    sums_ref,
    head_grads_ref,
    head_sums_ref,
    part_ref,
    grad_mixture_ref,
):
    step = pl.program_id(0)
    width = query_ref.shape[1]

    @pl.when(step == 0)
    def _():
        norm_grad, gain_sum, shift_sum = norm_back(
            both(own_ref, other_ref), hidden_ref[...], row_of(table_ref, CROSS_GAIN)
        )
        grad = grad_two_ref[...] + norm_grad
        grad_ref[...] = grad
        sums_ref[0:1, :] = gain_sum
        sums_ref[1:2, :] = shift_sum
        sums_ref[2:3, :] = jnp.sum(grad, axis=0, keepdims=True)
        rounded = grad.astype(BF16)
        rounded_ref[...] = rounded
        grad_mixture_ref[...] = dot(rounded, mixer_ref[...], NT).astype(BF16)

    grads = attend_pair_back(
        pair_columns(grad_mixture_ref, 0, step),
        pair_columns(heads_ref, 0, step),
        pair_columns(heads_ref, width, step),
        pair_columns(heads_ref, 2 * width, step),
        pair_columns(mixture_ref, 0, step),
        weights_ref,
        inverse_ref,
    )
    for index, grad_heads in enumerate(grads):
        columns = pl.ds(pl.multiple_of(index * width + step * PAIR, PAIR), PAIR)
        head_grads_ref[:, columns] = grad_heads
        head_sums_ref[0:1, columns] = jnp.sum(grad_heads.astype(F32), axis=0, keepdims=True)

    @pl.when(step == pl.num_programs(0) - 1)
    def _():
        part = dot(head_grads_ref[:, :width], query_ref[...], NT)
        part = part + dot(head_grads_ref[:, width : 2 * width], key_ref[...], NT)
        part = part + dot(head_grads_ref[:, 2 * width :], value_ref[...], NT)
        part_ref[...] = part.astype(BF16)


def self_backward(
    grad_two, own, other, hidden, table, query, key, value, mixer, heads, mixture, weights, inverse
):
    length, model = grad_two.shape
    width = query.shape[1]
    pairs = width // PAIR
    arrays = (grad_two, own, other, hidden, table, query, key, value, mixer, heads, mixture)
    return call(
        self_backward_kernel,
        (pairs,),
        [whole(x.shape) for x in arrays]
        + [
            pl.BlockSpec((2, length, length), lambda g: (g, 0, 0)),
            pl.BlockSpec((2, length, 1), lambda g: (g, 0, 0)),
        ],
        [
            ((length, model), F32, whole((length, model))),
            ((length, model), BF16, whole((length, model))),
            ((8, model), F32, whole((8, model))),
            ((length, 3 * width), BF16, whole((length, 3 * width))),
            ((8, 3 * width), F32, whole((8, 3 * width))),
            ((length, model), BF16, whole((length, model))),
        ],
        scratch=[pltpu.VMEM((length, width), BF16)],
        flops=8 * length * model * width + 64 * pairs * length * length * PAIR,
        traffic=8 * model * width + 24 * length * model,
        name="self_backward",
    )(*arrays, weights, inverse)


def output_kernel(clips, *refs):
    table_ref, out_ref = refs[3 * clips], refs[3 * clips + 1]
    for clip in range(clips):
        hidden_ref, own_ref, other_ref = refs[3 * clip : 3 * clip + 3]
        out_ref[clip] = hidden_ref[...] + both(own_ref, other_ref) + row_of(table_ref, REDUCE_BIAS)


def layer_output(hidden, own, other, table):
    clips = len(hidden)
    length, model = hidden[0].shape
    rows = length // 4
    block = pl.BlockSpec((rows, model), lambda g: (g, 0))
    args = [x for clip in range(clips) for x in (hidden[clip], own[clip], other[clip])]
    (out,) = call(
        functools.partial(output_kernel, clips),
        (4,),
        [block] * len(args) + [whole(table.shape)],
        [
            (
                (clips, length, model),
                F32,
                pl.BlockSpec((clips, rows, model), lambda g: (0, g, 0)),
            )
        ],
        flops=4 * clips * length * model,
        traffic=12 * clips * length * model,
        name="layer_output",
    )(*args, table)
    return out


def token_grad_kernel(clips, tokens_ref, *refs):
    table_ref, out_ref, sums_ref = refs[3 * clips :]

    @pl.when(pl.program_id(0) == 0)
    def _():
        sums_ref[...] = jnp.zeros_like(sums_ref)

    for clip in range(clips):
        grad_ref, own_ref, other_ref = refs[3 * clip : 3 * clip + 3]
        norm_grad, gain_sum, shift_sum = norm_back(
            both(own_ref, other_ref), tokens_ref[clip].astype(F32), row_of(table_ref, SELF_GAIN)
        )
        out_ref[clip] = grad_ref[...] + norm_grad
        sums_ref[0:1, :] += gain_sum
        sums_ref[1:2, :] += shift_sum


def token_grad(tokens, grad_one, own, other, table):
    clips, length, model = tokens.shape
    rows = length // 4
    block = pl.BlockSpec((rows, model), lambda g: (g, 0))
    clip_rows = pl.BlockSpec((clips, rows, model), lambda g: (0, g, 0))
    args = [x for clip in range(clips) for x in (grad_one[clip], own[clip], other[clip])]
    return call(
        functools.partial(token_grad_kernel, clips),
        (4,),
        [clip_rows] + [block] * len(args) + [whole(table.shape)],
        [
            ((clips, length, model), F32, clip_rows),
            ((8, model), F32, whole((8, model))),
        ],
        flops=20 * clips * length * model,
        traffic=14 * clips * length * model,
        name="token_grad",
    )(tokens, *args, table)


def weight_grad_kernel(clips, where_ref, *refs):
    send_ref, keep_ref = refs[2 * clips :]
    half = send_ref.shape[0]
    core = where_ref[0]

    def total_of(columns):
        total = None
        for clip in range(clips):
            left_ref, right_ref = refs[2 * clip : 2 * clip + 2]
            part = dot(left_ref[:, columns], right_ref[...], TN)
            total = part if total is None else total + part
        return total.astype(BF16)

    if half % 128 == 0:
        send_ref[...] = total_of(pl.ds(pl.multiple_of((1 - core) * half, 128), half))
        keep_ref[...] = total_of(pl.ds(pl.multiple_of(core * half, 128), half))
    else:
        total = total_of(slice(None)).astype(F32)
        low, high = total[:half], total[half:]
        send_ref[...] = jnp.where(core == 0, high, low).astype(BF16)
        keep_ref[...] = jnp.where(core == 0, low, high).astype(BF16)


def weight_grad(where, left, right, tile):
    clips = len(left)
    length, rows = left[0].shape
    columns = right[0].shape[-1]
    tile = min(tile, columns)
    half = rows // 2
    out = pl.BlockSpec((half, tile), lambda g, where: (0, g))
    in_specs, args = [], []
    for clip in range(clips):
        in_specs.append(pl.BlockSpec((length, rows), lambda g, where: (0, 0)))
        args.append(left[clip])
        if right[clip].ndim == 3:
            in_specs.append(
                pl.BlockSpec((None, length, tile), lambda g, where, clip=clip: (clip, 0, g))
            )
        else:
            in_specs.append(pl.BlockSpec((length, tile), lambda g, where: (0, g)))
        args.append(right[clip])
    return pl.pallas_call(
        functools.partial(weight_grad_kernel, clips),
        grid_spec=pltpu.PrefetchScalarGridSpec(
            num_scalar_prefetch=1,
            grid=(columns // tile,),
            in_specs=in_specs,
            out_specs=[out, out],
        ),
        out_shape=[jax.ShapeDtypeStruct((half, columns), BF16)] * 2,
        cost_estimate=pl.CostEstimate(
            flops=2 * clips * length * rows * columns,
            bytes_accessed=2 * (clips * length * (rows + columns) + rows * columns),
            transcendentals=0,
        ),
        name="weight_grad",
    )(where, *args)


def frame_weight_grad_kernel(clips, frames, where_ref, encoded_ref, *refs):
    send_ref, keep_ref, total_ref = refs[2 * clips :]
    clip, block = pl.program_id(0), pl.program_id(1)
    rows = encoded_ref.shape[0]
    row = lax.broadcasted_iota(jnp.int32, (rows, 1), 0) + block * rows
    encoded = jnp.where(row < frames, encoded_ref[...], 0)
    width = refs[0].shape[1]

    @pl.when((clip == 0) & (block == 0))
    def _():
        total_ref[...] = jnp.zeros_like(total_ref)

    for index in range(clips):

        @pl.when(clip == index)
        def _():
            total_ref[:, :width] += dot(encoded, refs[2 * index][...], TN)
            total_ref[:, width:] += dot(encoded, refs[2 * index + 1][...], TN)

    @pl.when((clip == clips - 1) & (block == pl.num_programs(1) - 1))
    def _():
        core = where_ref[0]
        half = send_ref.shape[0]
        send_ref[...] = total_ref[pl.ds(pl.multiple_of((1 - core) * half, 8), half), :].astype(BF16)
        keep_ref[...] = total_ref[pl.ds(pl.multiple_of(core * half, 8), half), :].astype(BF16)


def frame_weight_grad(where, encoded, key_grads, value_grads):
    clips, frames, model = encoded.shape
    width = key_grads[0].shape[1]
    blocks = -(-frames // FRAME_ROWS)
    half = pl.BlockSpec((model // 2, 2 * width), lambda c, r, where: (0, 0))
    in_specs = [pl.BlockSpec((None, FRAME_ROWS, model), lambda c, r, where: (c, r, 0))]
    args = []
    for clip in range(clips):

        def rows_of(c, r, where, clip=clip):
            return (jnp.where(c == clip, r, jnp.where(c < clip, 0, blocks - 1)), 0)

        in_specs += [pl.BlockSpec((FRAME_ROWS, width), rows_of)] * 2
        args += [key_grads[clip], value_grads[clip]]
    return pl.pallas_call(
        functools.partial(frame_weight_grad_kernel, clips, frames),
        grid_spec=pltpu.PrefetchScalarGridSpec(
            num_scalar_prefetch=1,
            grid=(clips, blocks),
            in_specs=in_specs,
            out_specs=[half, half],
            scratch_shapes=[pltpu.VMEM((model, 2 * width), F32)],
        ),
        out_shape=[jax.ShapeDtypeStruct((model // 2, 2 * width), BF16)] * 2,
        cost_estimate=pl.CostEstimate(
            flops=4 * clips * frames * model * width,
            bytes_accessed=2 * clips * frames * (model + 2 * width),
            transcendentals=0,
        ),
        name="frame_weight_grad",
    )(where, encoded, *args)


def frame_terms_kernel(where_ref, key_grad_ref, value_grad_ref, key_ref, value_ref, out_ref):
    terms = dot(key_grad_ref[...], key_ref[...], NT)
    terms = terms + dot(value_grad_ref[...], value_ref[...], NT)
    out_ref[...] = terms.astype(out_ref.dtype)


def frame_total_kernel(
    where_ref, key_grad_ref, value_grad_ref, key_ref, value_ref, other_ref, *refs
):
    terms = dot(key_grad_ref[...], key_ref[...], NT)
    terms = terms + dot(value_grad_ref[...], value_ref[...], NT)
    refs[-1][...] = terms + other_ref[...].astype(F32)


def frame_grad(clip, clips, frames, where, key_grad, value_grad, key, value, share, other, total):
    width = key.shape[1]
    blocks = -(-frames // FRAME_ROWS)
    sent = other is None
    rows = pl.BlockSpec((FRAME_ROWS, width), lambda r, where: (r, 0))
    side = 2 if sent else 1
    weight = pl.BlockSpec((share, width), lambda r, where: (where[side], 0))
    features = pl.BlockSpec((FRAME_ROWS, share), lambda r, where: (r, 0))
    in_specs = [rows, rows, weight, weight]
    args = [key_grad, value_grad, key, value]
    aliases = {}
    if sent:
        out_shape = jax.ShapeDtypeStruct((frames, share), BF16)
        out_spec = features
    else:
        in_specs.append(features)
        args.append(other)
        out_shape = jax.ShapeDtypeStruct((clips, frames, share), F32)
        out_spec = pl.BlockSpec((None, FRAME_ROWS, share), lambda r, where: (clip, r, 0))
        if total is not None:
            in_specs.append(pl.BlockSpec(memory_space=pl.ANY))
            args.append(total)
            aliases = {len(args): 0}
    return pl.pallas_call(
        frame_terms_kernel if sent else frame_total_kernel,
        grid_spec=pltpu.PrefetchScalarGridSpec(
            num_scalar_prefetch=1,
            grid=(blocks,),
            in_specs=in_specs,
            out_specs=out_spec,
        ),
        out_shape=out_shape,
        input_output_aliases=aliases,
        cost_estimate=pl.CostEstimate(
            flops=4 * frames * share * width,
            bytes_accessed=4 * frames * (share + width),
            transcendentals=0,
        ),
        name="frame_terms" if sent else "frame_total",
    )(where, *args)


def place_kernel(layers, tiles, where, *refs):
    ins, outs = refs[:4], refs[4:]
    core, row, layer = where[0], where[3], where[4]
    quarter = ins[0].shape[0]
    block = quarter // layers

    def put(out_ref):
        for index, ref in enumerate(ins):
            base = (
                jnp.bitwise_xor(core, index // 2) * 2 + jnp.bitwise_xor(row, index % 2)
            ) * quarter
            for step in range(layers):
                at = base + lax.rem(layer + layers - step, layers) * block
                out_ref[pl.ds(pl.multiple_of(at, 8), block), :] = ref[
                    step * block : (step + 1) * block, :
                ].astype(F32)

    for index, out_ref in enumerate(outs):

        @pl.when(pl.program_id(0) // tiles == index)
        def _():
            put(out_ref)


def place(where, layers, quarters, outputs):
    quarter, width = quarters[0].shape
    part = width // outputs
    tile = min(256, part)
    tiles = part // tile

    def column_of(index):
        return lambda g, where: (0, jnp.clip(g - index * tiles, 0, tiles - 1))

    return pl.pallas_call(
        functools.partial(place_kernel, layers, tiles),
        out_shape=[jax.ShapeDtypeStruct((4 * quarter, part), F32)] * outputs,
        grid_spec=pltpu.PrefetchScalarGridSpec(
            num_scalar_prefetch=1,
            grid=(width // tile,),
            in_specs=[pl.BlockSpec((quarter, tile), lambda g, where: (0, g))] * 4,
            out_specs=[
                pl.BlockSpec((4 * quarter, tile), column_of(index)) for index in range(outputs)
            ],
        ),
        cost_estimate=pl.CostEstimate(
            flops=4 * quarter * width, bytes_accessed=24 * quarter * width, transcendentals=0
        ),
        name="place",
    )(where, *quarters)


def dp_sum(where, send, keep, outputs=1):
    devices = lax.axis_size("dp")
    half = keep.shape[0]
    layers = devices // 4
    me = lax.axis_index("dp")
    core, row, layer = me % 2, (me // 2) % 2, me // 4
    across_core = [(i, i ^ 1) for i in range(devices)]
    across_row = [(i, i ^ 2) for i in range(devices)]
    along = [(i, (i + 4) % devices) for i in range(devices)]
    quarter, block = half // 2, half // (2 * layers)
    if devices % 4 or half % (32 * layers):
        low, high = jnp.where(core == 0, keep, send), jnp.where(core == 0, send, keep)
        total = lax.psum(jnp.concatenate([low, high]).astype(F32), "dp")
        return jnp.split(total, outputs, axis=1)

    def cut(values, start, size):
        return lax.dynamic_slice_in_dim(values, start, size, 0)

    def add(left, right):
        return (left.astype(F32) + right.astype(F32)).astype(BF16)

    got = lax.ppermute(send, "dp", across_core)

    def pair(at):
        return add(cut(keep, at * quarter, quarter), cut(got, at * quarter, quarter))

    total = add(pair(row), lax.ppermute(pair(1 - row), "dp", across_row))
    carry = cut(total, ((layer + layers - 1) % layers) * block, block)
    for step in range(layers - 1):
        carry = add(
            lax.ppermute(carry, "dp", along),
            cut(total, ((layer + 2 * layers - 2 - step) % layers) * block, block),
        )
    pieces = [carry]
    for step in range(layers - 1):
        pieces.append(lax.ppermute(pieces[-1], "dp", along))
    mine = jnp.concatenate(pieces, axis=0)
    other = lax.ppermute(mine, "dp", across_row)
    quarters = [
        mine,
        other,
        lax.ppermute(mine, "dp", across_core),
        lax.ppermute(other, "dp", across_core),
    ]
    return place(where, layers, quarters, outputs)


def dp_sum_vector(values):
    devices = lax.axis_size("dp")
    if devices & (devices - 1):
        return lax.psum(values, "dp")
    step = 1
    while step < devices:
        pairs = [(i, i ^ step) for i in range(devices)]
        values = values + lax.ppermute(values, "dp", pairs)
        step = 2 * step
    return values


def tensor_terms(mine):
    if lax.axis_size("tensor") == 2:
        return mine, lax.ppermute(mine, "tensor", [(0, 1), (1, 0)])
    return lax.psum(mine.astype(F32), "tensor").astype(BF16), jnp.zeros_like(mine)


def local(
    tokens,
    encoded,
    cotangent,
    self_gain,
    self_shift,
    self_query,
    self_query_bias,
    self_key,
    self_value,
    self_value_bias,
    self_mixer,
    self_mixer_bias,
    cross_gain,
    cross_shift,
    cross_query,
    cross_query_bias,
    cross_key,
    cross_value,
    cross_value_bias,
    cross_mixer,
    cross_mixer_bias,
    feed_gain,
    feed_shift,
    expand_weight,
    expand_bias,
    reduce_weight,
    reduce_bias,
):
    clips, length, width = tokens.shape
    frames = encoded.shape[1]
    local_width = self_query.shape[1]
    members = lax.axis_size("tensor")
    each = range(clips)
    device = lax.axis_index("dp")
    member = lax.axis_index("tensor")
    where = jnp.stack(
        [device % 2, member, (member + 1) % members, (device // 2) % 2, device // 4]
    ).astype(jnp.int32)
    table = jnp.stack(
        [
            self_gain,
            self_shift,
            self_mixer_bias,
            cross_gain,
            cross_shift,
            cross_mixer_bias,
            feed_gain,
            feed_shift,
            reduce_bias,
        ]
    ).astype(F32)
    biases = jnp.stack(
        [self_query_bias, self_value_bias, cross_query_bias, cross_value_bias]
    ).astype(F32)
    expand_row = expand_bias.astype(F32).reshape(1, -1)

    selves = [
        self_forward(
            i, tokens, table, biases, self_query, self_key, self_value, self_mixer
        )
        for i in each
    ]
    attn_in, self_heads, self_mixture, self_weights, self_inverse, self_part = zip(*selves)
    self_terms = [tensor_terms(self_part[i]) for i in each]
    heads = frame_heads(encoded, cross_key, cross_value, biases)

    crosses = [
        cross_forward(
            i, frames, tokens, *self_terms[i], table, biases, cross_query, cross_mixer, heads
        )
        for i in each
    ]
    hidden_one, cross_in, cross_queries, cross_mixture, cross_weights, cross_inverse, cross_part = (
        zip(*crosses)
    )
    cross_terms = [tensor_terms(cross_part[i]) for i in each]

    feeds = [
        feed(
            i,
            cotangent,
            hidden_one[i],
            *cross_terms[i],
            table,
            expand_weight,
            expand_row,
            reduce_weight,
        )
        for i in each
    ]
    hidden_two, feed_in, activated, grad_preact, expand_sum, cot_sum, feed_part, feed_grad_part = (
        zip(*feeds)
    )
    feed_grad_terms = [tensor_terms(feed_grad_part[i]) for i in each]
    (grad_reduce_weight,) = dp_sum(where, *weight_grad(where, activated, [cotangent] * clips, 512))
    (grad_expand_weight,) = dp_sum(where, *weight_grad(where, feed_in, grad_preact, 512))
    feed_terms = [tensor_terms(feed_part[i]) for i in each]

    cross_backs = [
        cross_backward(
            i,
            frames,
            cotangent,
            *feed_grad_terms[i],
            hidden_two[i],
            table,
            cross_query,
            cross_mixer,
            cross_queries[i],
            cross_mixture[i],
            heads,
            cross_weights[i],
            cross_inverse[i],
        )
        for i in each
    ]
    (
        grad_two,
        two_rounded,
        feed_sums,
        query_grad,
        key_grad,
        value_grad,
        cross_head_sums,
        cross_grad_part,
    ) = zip(*cross_backs)
    cross_grad_terms = [tensor_terms(cross_grad_part[i]) for i in each]
    (grad_cross_mixer,) = dp_sum(where, *weight_grad(where, cross_mixture, two_rounded, 512))
    (grad_cross_query,) = dp_sum(where, *weight_grad(where, cross_in, query_grad, 512))
    grad_cross_key, grad_cross_value = dp_sum(
        where, *frame_weight_grad(where, encoded, key_grad, value_grad), 2
    )

    self_backs = [
        self_backward(
            grad_two[i],
            *cross_grad_terms[i],
            hidden_one[i],
            table,
            self_query,
            self_key,
            self_value,
            self_mixer,
            self_heads[i],
            self_mixture[i],
            self_weights[i],
            self_inverse[i],
        )
        for i in each
    ]
    grad_one, one_rounded, cross_sums, head_grads, self_head_sums, self_grad_part = zip(*self_backs)
    self_grad_terms = [tensor_terms(self_grad_part[i]) for i in each]
    (grad_self_mixer,) = dp_sum(where, *weight_grad(where, self_mixture, one_rounded, 512))
    grad_self_query, grad_self_key, grad_self_value = dp_sum(
        where, *weight_grad(where, attn_in, head_grads, 512), 3
    )

    share = width // members
    if members == 2:
        grad_encoded = None
        for i in each:
            args = (where, key_grad[i], value_grad[i], cross_key, cross_value, share)
            sent = frame_grad(i, clips, frames, *args, None, None)
            other = lax.ppermute(sent, "tensor", [(0, 1), (1, 0)])
            grad_encoded = frame_grad(i, clips, frames, *args, other, grad_encoded)
    else:
        terms = [
            jnp.einsum("lc,dc->ld", key_grad[i], cross_key, preferred_element_type=F32)
            + jnp.einsum("lc,dc->ld", value_grad[i], cross_value, preferred_element_type=F32)
            for i in each
        ]
        grad_encoded = jnp.stack(
            [
                lax.psum_scatter(terms[i][:frames], "tensor", scatter_dimension=1, tiled=True)
                for i in each
            ]
        )

    output = layer_output(
        hidden_two, [x[0] for x in feed_terms], [x[1] for x in feed_terms], table
    )
    grad_tokens, self_sums = token_grad(
        tokens, grad_one, [x[0] for x in self_grad_terms], [x[1] for x in self_grad_terms], table
    )

    feed_sums, cross_sums, expand_sum, cot_sum = (
        sum(x) for x in (feed_sums, cross_sums, expand_sum, cot_sum)
    )
    cross_head_sums, self_head_sums = sum(cross_head_sums), sum(self_head_sums)
    vectors = [
        self_sums[0],
        self_sums[1],
        cross_sums[2],
        cross_sums[0],
        cross_sums[1],
        feed_sums[2],
        feed_sums[0],
        feed_sums[1],
        cot_sum[0],
        self_head_sums[0, :local_width],
        self_head_sums[0, 2 * local_width :],
        cross_head_sums[0],
        cross_head_sums[1],
        expand_sum[0],
    ]
    summed = dp_sum_vector(jnp.concatenate(vectors))
    pieces, offset = [], 0
    for piece in vectors:
        pieces.append(summed[offset : offset + piece.size])
        offset = offset + piece.size
    return (
        output,
        grad_tokens,
        grad_encoded,
        pieces[0],
        pieces[1],
        grad_self_query,
        pieces[9],
        grad_self_key,
        grad_self_value,
        pieces[10],
        grad_self_mixer,
        pieces[2],
        pieces[3],
        pieces[4],
        grad_cross_query,
        pieces[11],
        grad_cross_key,
        grad_cross_value,
        pieces[12],
        grad_cross_mixer,
        pieces[5],
        pieces[6],
        pieces[7],
        grad_expand_weight,
        pieces[13],
        grad_reduce_weight,
        pieces[8],
    )


def solution(mesh):
    rows = P("dp", None, None)
    column, row, part = P(None, "tensor"), P("tensor", None), P("tensor")
    return jax.shard_map(
        local,
        mesh=mesh,
        in_specs=(
            rows,
            rows,
            rows,
            P(),
            P(),
            column,
            part,
            column,
            column,
            part,
            row,
            P(),
            P(),
            P(),
            column,
            part,
            column,
            column,
            part,
            row,
            P(),
            P(),
            P(),
            column,
            part,
            row,
            P(),
        ),
        out_specs=(
            rows,
            rows,
            P("dp", None, "tensor"),
            P(),
            P(),
            column,
            part,
            column,
            column,
            part,
            row,
            P(),
            P(),
            P(),
            column,
            part,
            column,
            column,
            part,
            row,
            P(),
            P(),
            P(),
            column,
            part,
            row,
            P(),
        ),
        check_vma=False,
    )
```
